32 devices in a mesh: space: 8 (over y, x, core), vec: 4 (over z).
Axes of the slice: x: 2, y: 2, z: 4, core: 2. Of those that a mesh axis runs over, the one named last changes fastest.
Arguments:
- vectors: float32 [2, 3, 384, 8, 2048], P(None, None, 'vec', 'space'), may hold values from -0.375 to 0.375
- links: float32 [3, 2, 3, 3, 8, 2048], P(None, None, None, None, 'space'), may hold values from -3.5 to 3.5
- momenta: int32 [2, 3], replicated, may hold values from -2 to 2
- directions: int32 [3], replicated, may hold values from 0 to 2, each once
Outputs:
- elementals: float32 [2, 3, 2, 384, 384], P(None, None, None, 'space', 'vec')
The draws below stay inside these ranges and needn't reach their ends.
Inputs may be any that keep to these rules, and one draw needn't show every extreme that they name: directions holds each of 0, 1, 2 once.
All inputs are finite; a program needn't handle non-finite values.
Results may differ from the reference program's by a relative error of at most 0.000098.
Values sent between devices are 32-bit elements; how exact they have to be, the bound alone decides.
No kernel may reach another device: no remote copies, remote signals or barrier semaphores. Data moves between devices by JAX's collectives and lax.ppermute only.
A program may use at most 128 MiB of HBM per device.

```python
import jax
import jax.numpy as jnp
from jax import lax

NV = 384
LY = 32
LZ = 64
NMOM = 2
LX = 8


def plant(entries, own_key, low, high):
    longest = entries.shape.index(max(entries.shape))
    spots = []
    for shift in (0, 1):
        where = [jax.random.randint(jax.random.fold_in(own_key, axis), (), 0, length) for axis, length in enumerate(entries.shape)]
        where[longest] = (where[longest] + shift) % entries.shape[longest]
        spots.append(tuple(where))
    return entries.at[spots[0]].set(low).at[spots[1]].set(high)


def block_levels(own_key, dims, pieces, low, largest):
    level = 1.0
    for dim, parts in pieces:
        draws = jax.random.uniform(jax.random.fold_in(jax.random.fold_in(own_key, 6), dim), (parts,), jnp.float32, low / len(pieces), largest / len(pieces))
        level = level * jnp.repeat(jnp.exp(draws), dims[dim] // parts).reshape((-1,) + (1,) * (len(dims) - 1 - dim))
    return level


def bell_draw(rng, extent, deviation, most, shards=(), kind=jnp.bfloat16):
    values = deviation * jax.random.normal(rng, extent, jnp.float32)
    if shards:
        values = values * block_levels(rng, extent, shards, -0.22, 0.18)
    return jnp.clip(values, -most, most).astype(kind)


def setup_inputs(seed: int = 0) -> dict:
    seeds = jax.random.split(jax.random.key(seed), 5)
    vectors = bell_draw(seeds[0], (2, 3, NV, LX, LY * LZ), 0.06, 0.375, ((2, 4), (3, 8)), jnp.float32)
    links = bell_draw(seeds[1], (3, 2, 3, 3, LX, LY * LZ), 0.577, 3.5, ((4, 8),), jnp.float32)
    momenta = plant(jax.random.randint(seeds[2], (NMOM, 3), -2, 3), jax.random.fold_in(seeds[2], 1), -2, 2).astype(jnp.int32)
    directions = jax.random.permutation(seeds[3], 3).astype(jnp.int32)
    return dict(vectors=vectors, links=links, momenta=momenta, directions=directions)


def site_shift(field, mu, step):
    if mu == 0:
        return jnp.roll(field, -step, axis=-2)
    shape = field.shape
    cube = field.reshape(shape[:-1] + (LY, LZ))
    cube = jnp.roll(cube, -step, axis=-3 + mu)
    return cube.reshape(shape)


def color_apply(link, field, dagger):
    link_re = link[0]
    link_im = link[1]
    if dagger:
        link_re = jnp.swapaxes(link_re, 0, 1)
        link_im = -jnp.swapaxes(link_im, 0, 1)
    link_re = link_re[:, :, None]
    link_im = link_im[:, :, None]
    field_re = field[0][None]
    field_im = field[1][None]
    out_re = jnp.sum(link_re * field_re - link_im * field_im, axis=1)
    out_im = jnp.sum(link_re * field_im + link_im * field_re, axis=1)
    return jnp.stack([out_re, out_im], 0)


def displace(vectors, links, mu):
    forward = color_apply(links[mu], site_shift(vectors, mu, 1), False)
    backward = site_shift(color_apply(links[mu], vectors, True), mu, -1)
    return forward - backward


def phase_tables(momenta, xcoord, sites):
    ycoord = sites // LZ
    zcoord = sites % LZ
    p0 = momenta[:, 0][:, None, None]
    p1 = momenta[:, 1][:, None, None]
    p2 = momenta[:, 2][:, None, None]
    frac = ((p0 * xcoord[None]) % LX).astype(jnp.float32) / LX
    frac = frac + ((p1 * ycoord[None, None]) % LY).astype(jnp.float32) / LY
    frac = frac + ((p2 * zcoord[None, None]) % LZ).astype(jnp.float32) / LZ
    theta = 2.0 * jnp.pi * frac
    return jnp.cos(theta), jnp.sin(theta)


def elemental_block(left_vecs, right_disp, cosine, sine):
    vec_re = left_vecs[0][None]
    vec_im = left_vecs[1][None]
    cosine = cosine[:, None, None]
    sine = sine[:, None, None]
    left_re = vec_re * cosine - vec_im * sine
    left_im = -(vec_re * sine + vec_im * cosine)
    left = jnp.stack([left_re, left_im], 1)
    gram = jnp.einsum("mpcaxs,dqcbxs->mpadqb", left, right_disp, precision=lax.Precision.HIGHEST, preferred_element_type=jnp.float32)
    part_re = gram[:, 0, :, :, 0] - gram[:, 1, :, :, 1]
    part_im = gram[:, 0, :, :, 1] + gram[:, 1, :, :, 0]
    stacked = jnp.stack([part_re, part_im], 1)
    return jnp.transpose(stacked, (0, 3, 1, 2, 4))


def reference(vectors, links, momenta, directions):
    displaced = jnp.stack([displace(vectors, links, mu) for mu in range(3)], 0)
    xcoord = jnp.arange(LX, dtype=jnp.int32)[:, None]
    sites = jnp.arange(LY * LZ, dtype=jnp.int32)
    cosine, sine = phase_tables(momenta, xcoord, sites)
    full = elemental_block(vectors, displaced, cosine, sine)
    return jnp.take(full, directions, axis=1)
```

```python
import functools

import jax
import jax.numpy as jnp
from jax import lax
from jax.experimental import pallas as pl
from jax.experimental.pallas import tpu as pltpu
from jax.sharding import PartitionSpec as P

LANES = 128
PLANE_Z = 64
TILE = 16
F32 = jnp.float32
BF16 = jnp.bfloat16


def xor_pairs(size, k):
    return [(i, i ^ k) for i in range(size)]


def bits_of(size):
    return size.bit_length() - 1


def split(value):
    high = value.astype(BF16)
    return high, (value - high.astype(F32)).astype(BF16)


def matvec(link, re, im, dagger):
    out_re, out_im = [], []
    for row in range(3):
        acc_re = acc_im = None
        for col in range(3):
            u_re, u_im = link[col * 3 + row] if dagger else link[row * 3 + col]
            if dagger:
                t_re = u_re * re[col] + u_im * im[col]
                t_im = u_re * im[col] - u_im * re[col]
            else:
                t_re = u_re * re[col] - u_im * im[col]
                t_im = u_re * im[col] + u_im * re[col]
            acc_re = t_re if acc_re is None else acc_re + t_re
            acc_im = t_im if acc_im is None else acc_im + t_im
        out_re.append(acc_re)
        out_im.append(acc_im)
    return out_re, out_im


def chunk_kernel(has_acc, nv, coef_ref, v_ref, vx_ref, row_ref, *refs):
    if has_acc:
        acc_ref, out_ref, left_v, left_w, left_r, right, right_r = refs
    else:
        out_ref, left_v, left_w, left_r, right, right_r = refs
        acc_ref = None

    @pl.when(pl.program_id(0) == 0)
    def _():
        lane = lax.broadcasted_iota(jnp.int32, (TILE, LANES), 1)
        low = lane < PLANE_Z
        at_end = lane % PLANE_Z == PLANE_Z - 1
        at_start = lane % PLANE_Z == 0

        def coef(index):
            return jnp.broadcast_to(coef_ref[pl.ds(index, 1), :], (TILE, LANES))

        def link_of(mu):
            return [
                (coef(mu * 18 + e), coef(mu * 18 + 9 + e)) for e in range(9)
            ]

        def put(ref, rows, col, value):
            high, rest = split(value)
            ref[0, rows, pl.ds(col * LANES, LANES)] = high
            ref[1, rows, pl.ds(col * LANES, LANES)] = rest

        def phased(ref, rows_of, re, im, base):
            for m in range(2):
                cos, sin = coef(base + 2 * m), coef(base + 2 * m + 1)
                for c in range(3):
                    p = re[c] * cos - im[c] * sin
                    q = re[c] * sin + im[c] * cos
                    p_hi, p_lo = split(p)
                    q_hi, q_lo = split(q)
                    for half, (pp, qq) in enumerate(((p_hi, q_hi), (p_lo, q_lo))):
                        ref[half, rows_of(2 * m), pl.ds(c * LANES, LANES)] = pp
                        ref[half, rows_of(2 * m), pl.ds((3 + c) * LANES, LANES)] = qq
                        ref[half, rows_of(2 * m + 1), pl.ds(c * LANES, LANES)] = -qq
                        ref[half, rows_of(2 * m + 1), pl.ds((3 + c) * LANES, LANES)] = pp

        def body(step, carry):
            start = pl.multiple_of(step * TILE, TILE)
            rows = pl.ds(start, TILE)

            def rows_of(part):
                return pl.ds(pl.multiple_of(part * nv + start, TILE), TILE)

            re = [v_ref[c, rows, :] for c in range(3)]
            im = [v_ref[3 + c, rows, :] for c in range(3)]
            phased(left_v, rows_of, re, im, 54)
            xre = [vx_ref[c, rows, :] for c in range(3)]
            xim = [vx_ref[3 + c, rows, :] for c in range(3)]
            wre, wim = matvec(link_of(0), xre, xim, False)
            phased(left_w, rows_of, wre, wim, 58)
            for c in range(3):
                put(right.at[0], rows, c, wre[c])
                put(right.at[0], rows, 3 + c, wim[c])
                put(right.at[3], rows, c, re[c])
                put(right.at[3], rows, 3 + c, im[c])
            packed = [row_ref[c, rows, :] for c in range(3)]
            turned = [pltpu.roll(packed[c], PLANE_Z, 1) for c in range(3)]
            link1 = link_of(1)
            fre = [jnp.where(low, pltpu.roll(re[c], PLANE_Z, 1), turned[c]) for c in range(3)]
            fim = [jnp.where(low, pltpu.roll(im[c], PLANE_Z, 1), packed[c]) for c in range(3)]
            fre, fim = matvec(link1, fre, fim, False)
            bre, bim = matvec(link1, re, im, True)
            for c in range(3):
                r_re = pltpu.roll(bre[c], PLANE_Z, 1)
                r_im = pltpu.roll(bim[c], PLANE_Z, 1)
                put(right.at[1], rows, c, jnp.where(low, fre[c], fre[c] - r_re))
                put(right.at[1], rows, 3 + c, jnp.where(low, fim[c], fim[c] - r_im))
                put(right_r, rows, c, -jnp.where(low, r_re, bim[c]))
            for part in range(4):
                a, b = coef(62 + 2 * part), coef(63 + 2 * part)
                for c in range(3):
                    n_re = jnp.where(low, packed[c], turned[c])
                    n_im = jnp.where(low, turned[c], packed[c])
                    put(left_r, rows_of(part), c, n_re * a + n_im * b)
            link2 = link_of(2)
            zre = [jnp.where(at_end, pltpu.roll(re[c], PLANE_Z - 1, 1), pltpu.roll(re[c], LANES - 1, 1)) for c in range(3)]
            zim = [jnp.where(at_end, pltpu.roll(im[c], PLANE_Z - 1, 1), pltpu.roll(im[c], LANES - 1, 1)) for c in range(3)]
            zre, zim = matvec(link2, zre, zim, False)
            bre, bim = matvec(link2, re, im, True)
            for c in range(3):
                r_re = jnp.where(at_start, pltpu.roll(bre[c], PLANE_Z + 1, 1), pltpu.roll(bre[c], 1, 1))
                r_im = jnp.where(at_start, pltpu.roll(bim[c], PLANE_Z + 1, 1), pltpu.roll(bim[c], 1, 1))
                put(right.at[2], rows, c, zre[c] - r_re)
                put(right.at[2], rows, 3 + c, zim[c] - r_im)
            return carry

        lax.fori_loop(0, nv // TILE, body, 0)

    part = pl.program_id(0)
    rows = pl.ds(pl.multiple_of(part * nv, nv), nv)

    def product(left, right_side):
        dims = (((1,), (1,)), ((), ()))
        total = None
        for i, j in ((0, 0), (0, 1), (1, 0)):
            term = lax.dot_general(
                left[i, rows, :], right_side[j], dims, preferred_element_type=F32
            )
            total = term if total is None else total + term
        return total

    for mu in range(3):
        total = product(left_v, right.at[mu])
        if mu == 0:
            total = total + product(left_w, right.at[3])
        if mu == 1:
            total = total + product(left_r, right_r)
        if has_acc:
            total = total + acc_ref[mu]
        out_ref[mu] = total


def chunk_call(coef, v, vx, row, acc):
    nv = v.shape[1]
    has_acc = acc is not None
    whole = lambda shape: pl.BlockSpec(shape, lambda i: (0,) * len(shape))
    tile = pl.BlockSpec((3, nv, nv), lambda i: (0, i, 0))
    args = [coef, v, vx, row] + ([acc] if has_acc else [])
    specs = [whole(a.shape) for a in args[:4]] + ([tile] if has_acc else [])
    wide = 6 * LANES
    flops = 3 * 2 * 4 * nv * nv * wide * 4
    return pl.pallas_call(
        functools.partial(chunk_kernel, has_acc, nv),
        out_shape=jax.ShapeDtypeStruct((3, 4 * nv, nv), F32),
        grid=(4,),
        in_specs=specs,
        out_specs=tile,
        scratch_shapes=[
            pltpu.VMEM((2, 4 * nv, wide), BF16),
            pltpu.VMEM((2, 4 * nv, wide), BF16),
            pltpu.VMEM((2, 4 * nv, wide // 2), BF16),
            pltpu.VMEM((4, 2, nv, wide), BF16),
            pltpu.VMEM((2, nv, wide // 2), BF16),
        ],
        input_output_aliases={4: 0} if has_acc else {},
        cost_estimate=pl.CostEstimate(
            flops=flops, bytes_accessed=24 * nv * nv, transcendentals=0
        ),
        compiler_params=pltpu.CompilerParams(vmem_limit_bytes=56 * 1024 * 1024),
        name="chunk",
    )(*args)


def phase_rows(momenta, xcoord, sites, extent_x, plane_y):
    ycoord = sites // PLANE_Z
    zcoord = sites % PLANE_Z
    p0, p1, p2 = (momenta[:, i][:, None] for i in range(3))
    frac = (p0 * xcoord % extent_x).astype(F32) / extent_x
    frac = frac + (p1 * ycoord[None] % plane_y).astype(F32) / plane_y
    frac = frac + (p2 * zcoord[None] % PLANE_Z).astype(F32) / PLANE_Z
    theta = 2.0 * jnp.pi * frac
    return jnp.cos(theta), jnp.sin(theta)


def coefficients(links, momenta, xcoord, start, subs, extent_x, plane):
    plane_y = plane // PLANE_Z
    width = subs * LANES
    rows = lax.dynamic_slice_in_dim(links.reshape(54, plane), start, width, 1)
    sites = start + jnp.arange(width, dtype=jnp.int32)
    cos, sin = phase_rows(momenta, xcoord, sites, extent_x, plane_y)
    cos_x, sin_x = phase_rows(momenta, xcoord + 1, sites, extent_x, plane_y)
    after = jnp.arange(subs, dtype=jnp.int32)[:, None] * LANES + LANES
    after = start + after + jnp.arange(LANES, dtype=jnp.int32)[None] % PLANE_Z
    cos_r, sin_r = phase_rows(
        momenta, xcoord, after.reshape(-1) % plane, extent_x, plane_y
    )
    low = jnp.arange(width) % LANES < PLANE_Z
    parts = [rows]
    for m in range(2):
        parts += [cos[m : m + 1], sin[m : m + 1]]
    for m in range(2):
        parts += [-cos_x[m : m + 1], -sin_x[m : m + 1]]
    for m in range(2):
        c, s = cos_r[m : m + 1], sin_r[m : m + 1]
        parts += [
            jnp.where(low, c, s),
            jnp.where(low, -s, c),
            jnp.where(low, -s, c),
            jnp.where(low, -c, -s),
        ]
    parts.append(jnp.zeros((2, width), F32))
    table = jnp.concatenate(parts, 0)
    return [table[:, i * LANES : (i + 1) * LANES] for i in range(subs)]


def scatter_step(value, axis_dim, mine, axis, bit, size):
    keep = lax.dynamic_index_in_dim(value, mine, axis_dim, keepdims=False)
    send = lax.dynamic_index_in_dim(value, 1 - mine, axis_dim, keepdims=False)
    return keep + lax.ppermute(send, axis, xor_pairs(size, bit))


def reduce_block(block, order, n_space, n_vec):
    s = lax.axis_index("space")
    t = lax.axis_index("vec")
    s_bits, v_bits = bits_of(n_space), bits_of(n_vec)
    nv = block.shape[1]
    value = block.reshape((4,) + (2,) * s_bits + (nv // n_space, nv))
    left = list(range(s_bits))
    for level in order:
        mine = (s >> (s_bits - 1 - level)) & 1
        if level < v_bits:
            mine = mine ^ ((t >> (v_bits - 1 - level)) & 1)
        value = scatter_step(
            value, 1 + left.index(level), mine, "space", 1 << (s_bits - 1 - level), n_space
        )
        left.remove(level)
    width = nv // n_vec
    value = value.reshape(4, nv // n_space, n_vec, width)
    total = value[:, :, 0]
    for k in range(1, n_vec):
        total = total + lax.ppermute(value[:, :, k], "vec", xor_pairs(n_vec, k))
    return total


def on_device(vectors, links, momenta, directions):
    n_space, n_vec = lax.axis_size("space"), lax.axis_size("vec")
    s, t = lax.axis_index("space"), lax.axis_index("vec")
    own = vectors.shape[2]
    plane = vectors.shape[4]
    chunk = plane // n_vec
    subs = chunk // LANES
    field = vectors.reshape(6, own, plane)
    down = [(i, (i - 1) % n_space) for i in range(n_space)]

    def piece(k, sub):
        start = (t ^ k) * chunk + sub * LANES
        return lax.dynamic_slice_in_dim(field, start, LANES, 2)

    def first_row(k):
        start = (((t ^ k) + 1) % n_vec) * chunk
        row = lax.dynamic_slice_in_dim(field, start, PLANE_Z, 2)
        return jnp.concatenate([row[:3], row[3:]], 2)

    gather = lambda part: jnp.concatenate(
        [part(0)] + [lax.ppermute(part(k), "vec", xor_pairs(n_vec, k)) for k in range(1, n_vec)],
        1,
    )
    row = gather(first_row)
    tables = coefficients(links, momenta, s, t * chunk, subs, n_space * vectors.shape[3], plane)
    acc = None
    for sub in reversed(range(subs)):
        v = gather(lambda k: piece(k, sub))
        vx = lax.ppermute(v, "space", down)
        acc = chunk_call(tables[sub], v, vx, row, acc)
        row = jnp.concatenate([v[:3, :, :PLANE_Z], v[3:, :, :PLANE_Z]], 2)
    nv = own * n_vec
    s_bits = bits_of(n_space)
    forward = list(reversed(range(s_bits)))
    outs = []
    for mu in range(3):
        order = forward if mu != 1 else forward[:1] + list(reversed(forward[1:]))
        outs.append(reduce_block(acc[mu].reshape(4, nv, nv), order, n_space, n_vec))
    out = jnp.stack(outs, 0)
    out = jnp.take(out, directions, axis=0)
    out = out.reshape((3, 2, 2) + out.shape[2:])
    return jnp.transpose(out, (1, 0, 2, 3, 4))


def solution(mesh):
    placed = (
        P(None, None, "vec", "space", None),
        P(None, None, None, None, "space", None),
        P(),
        P(),
    )
    return jax.shard_map(
        on_device,
        mesh=mesh,
        in_specs=placed,
        out_specs=P(None, None, None, "space", "vec"),
        check_vma=False,
    )
```

```python
import functools

import jax
import jax.numpy as jnp
from jax import lax
from jax.experimental import pallas as pl
from jax.experimental.pallas import tpu as pltpu
from jax.sharding import PartitionSpec as P


LANES = 128
PLANE_Z = 64
TILE = 16
COLS = 256
F32 = jnp.float32
BF16 = jnp.bfloat16


def xor_pairs(size, k):
    return [(i, i ^ k) for i in range(size)]


def bits_of(size):
    return size.bit_length() - 1


def split(value):
    high = value.astype(BF16)
    return high, (value - high.astype(F32)).astype(BF16)


def matvec(link, re, im, dagger):
    out_re, out_im = [], []
    for row in range(3):
        acc_re = acc_im = None
        for col in range(3):
            u_re, u_im = link[col * 3 + row] if dagger else link[row * 3 + col]
            if dagger:
                t_re = u_re * re[col] + u_im * im[col]
                t_im = u_re * im[col] - u_im * re[col]
            else:
                t_re = u_re * re[col] - u_im * im[col]
                t_im = u_re * im[col] + u_im * re[col]
            acc_re = t_re if acc_re is None else acc_re + t_re
            acc_im = t_im if acc_im is None else acc_im + t_im
        out_re.append(acc_re)
        out_im.append(acc_im)
    return out_re, out_im


def tools_of(coef_ref):
    def coef(index):
        return jnp.broadcast_to(coef_ref[pl.ds(index, 1), :], (TILE, LANES))

    def link_of(mu):
        return [(coef(mu * 18 + e), coef(mu * 18 + 9 + e)) for e in range(9)]

    def phased(ref, nv, start, re, im, base):
        for m in range(2):
            cos, sin = coef(base + 2 * m), coef(base + 2 * m + 1)
            rows = pl.ds(pl.multiple_of(m * nv + start, TILE), TILE)
            for c in range(3):
                put(ref, rows, c, re[c] * cos - im[c] * sin)
                put(ref, rows, 3 + c, re[c] * sin + im[c] * cos)

    return coef, link_of, phased


def put(ref, rows, col, value):
    high, rest = split(value)
    ref[0, rows, pl.ds(col * LANES, LANES)] = high
    ref[1, rows, pl.ds(col * LANES, LANES)] = rest


def put_right(ref, nv, start, re, im):
    real = pl.ds(pl.multiple_of(start, TILE), TILE)
    imag = pl.ds(pl.multiple_of(nv + start, TILE), TILE)
    for c in range(3):
        r, i = split(re[c]), split(im[c])
        low, high = pl.ds(c * LANES, LANES), pl.ds((3 + c) * LANES, LANES)
        for half in range(2):
            ref[half, real, low] = r[half]
            ref[half, real, high] = i[half]
            ref[half, imag, low] = i[half]
            ref[half, imag, high] = -r[half]


def collect(block_refs, held, sems):
    copies = []
    for k, ref in enumerate(block_refs):
        own = ref.shape[1]
        to = held.at[:, pl.ds(k * own, own), :]
        copies.append(pltpu.make_async_copy(ref, to, sems.at[k]))
        copies[-1].start()
    return copies


def product(left, right, rows):
    dims = (((1,), (1,)), ((), ()))
    total = None
    for i, j in ((0, 0), (0, 1), (1, 0)):
        term = lax.dot_general(
            left[i], right[j, rows, :], dims, preferred_element_type=F32
        )
        total = term if total is None else total + term
    return total


def finish(mine_ref, total, cols, keep_ref, send_ref):
    count, shard = keep_ref.shape[:2]
    parts = total.reshape(count, 2, shard, total.shape[1])
    first, second = parts[:, 0], parts[:, 1]
    flip = mine_ref[0] == 1
    keep_ref[:, :, cols] = jnp.where(flip, second, first)
    send_ref[:, :, cols] = jnp.where(flip, first, second)


def tiles(nv, tile_of, prepare=None):
    steps = 2 * nv // COLS
    share = nv // steps

    def body(step, carry):
        if prepare is not None:
            for i in range(share // TILE):
                prepare(pl.multiple_of(step * share + i * TILE, TILE))
        tile_of(pl.ds(pl.multiple_of(step * COLS, COLS), COLS))
        return carry

    lax.fori_loop(0, steps, body, 0)


def plane_kernel(n_vec, has_acc, last, packed, nv, mine_ref, coef_ref, *refs):
    refs = list(refs)
    blocks = [refs.pop(0) for _ in range(n_vec)]
    row_blocks = [refs.pop(0) for _ in range(n_vec)]
    acc_ref = refs.pop(0) if has_acc else None
    outs = [refs.pop(0) for _ in range(4 if last else 1)]
    held, held_row, left_v, left_r, right_1, right_2, right_r, sems, row_sems = refs
    coef, link_of, phased = tools_of(coef_ref)
    lane = lax.broadcasted_iota(jnp.int32, (TILE, LANES), 1)
    low = lane < PLANE_Z
    at_end = lane % PLANE_Z == PLANE_Z - 1
    at_start = lane % PLANE_Z == 0
    turn = lambda x, by: pltpu.roll(x, by, 1)

    def load(start):
        rows = pl.ds(start, TILE)
        return [held[c, rows, :] for c in range(3)], [held[3 + c, rows, :] for c in range(3)]

    def prepare_1(start):
        rows = pl.ds(start, TILE)
        re, im = load(start)
        phased(left_v, nv, start, re, im, 54)
        if packed:
            both = [held_row[c, rows, :] for c in range(3)]
            turned = [turn(x, PLANE_Z) for x in both]
            n_re = [jnp.where(low, both[c], turned[c]) for c in range(3)]
            n_im = [jnp.where(low, turned[c], both[c]) for c in range(3)]
        else:
            n_re = [held_row[c, rows, :] for c in range(3)]
            n_im = [held_row[3 + c, rows, :] for c in range(3)]
            n_re = [jnp.where(low, x, turn(x, PLANE_Z)) for x in n_re]
            n_im = [jnp.where(low, x, turn(x, PLANE_Z)) for x in n_im]
        link1 = link_of(1)
        fre = [jnp.where(low, turn(re[c], PLANE_Z), n_re[c]) for c in range(3)]
        fim = [jnp.where(low, turn(im[c], PLANE_Z), n_im[c]) for c in range(3)]
        fre, fim = matvec(link1, fre, fim, False)
        bre, bim = matvec(link1, re, im, True)
        r_re = [turn(x, PLANE_Z) for x in bre]
        r_im = [turn(x, PLANE_Z) for x in bim]
        put_right(
            right_1,
            nv,
            start,
            [jnp.where(low, fre[c], fre[c] - r_re[c]) for c in range(3)],
            [jnp.where(low, fim[c], fim[c] - r_im[c]) for c in range(3)],
        )
        imag = pl.ds(pl.multiple_of(nv + start, TILE), TILE)
        for c in range(3):
            put(right_r, rows, c, -jnp.where(low, r_re[c], bim[c]))
            put(right_r, imag, c, jnp.where(low, -r_im[c], bre[c]))
        for m in range(2):
            a, b = coef(62 + 2 * m), coef(63 + 2 * m)
            to = pl.ds(pl.multiple_of(m * nv + start, TILE), TILE)
            for c in range(3):
                put(left_r, to, c, n_re[c] * a + n_im[c] * b)

    def prepare_2(start):
        re, im = load(start)
        link2 = link_of(2)
        ahead = lambda x: jnp.where(at_end, turn(x, PLANE_Z - 1), turn(x, LANES - 1))
        back = lambda x: jnp.where(at_start, turn(x, PLANE_Z + 1), turn(x, 1))
        zre, zim = matvec(link2, [ahead(x) for x in re], [ahead(x) for x in im], False)
        bre, bim = matvec(link2, re, im, True)
        put_right(
            right_2,
            nv,
            start,
            [zre[c] - back(bre[c]) for c in range(3)],
            [zim[c] - back(bim[c]) for c in range(3)],
        )

    def store(total, cols, pair):
        if has_acc:
            total = total + acc_ref[0, :, cols]
        if last:
            finish(mine_ref, total, cols, *pair)
        else:
            outs[0][0, :, cols] = total

    @pl.when(pl.program_id(0) == 0)
    def _():
        copies = collect(blocks, held, sems) + collect(row_blocks, held_row, row_sems)
        for copy in copies:
            copy.wait()

        def body(step, carry):
            prepare_1(pl.multiple_of(step * TILE, TILE))
            return carry

        lax.fori_loop(0, nv // TILE, body, 0)
        tiles(
            nv,
            lambda cols: store(
                product(left_v, right_1, cols) + product(left_r, right_r, cols), cols, outs[:2]
            ),
            prepare_2,
        )

    @pl.when(pl.program_id(0) == 1)
    def _():
        tiles(nv, lambda cols: store(product(left_v, right_2, cols), cols, outs[2:]))


def cross_kernel(n_vec, has_acc, last, nv, mine_ref, coef_ref, *refs):
    refs = list(refs)
    blocks = [refs.pop(0) for _ in range(n_vec)]
    next_blocks = [refs.pop(0) for _ in range(n_vec)]
    acc_ref = refs.pop(0) if has_acc else None
    outs = [refs.pop(0) for _ in range(2 if last else 1)]
    held, held_next, left_v, left_w, right_w, right_v, forward, sems, next_sems = refs
    _, link_of, phased = tools_of(coef_ref)

    def load(ref, start):
        rows = pl.ds(start, TILE)
        return [ref[c, rows, :] for c in range(3)], [ref[3 + c, rows, :] for c in range(3)]

    def prepare_1(start):
        re, im = load(held, start)
        phased(left_v, nv, start, re, im, 54)
        re, im = load(held_next, start)
        re, im = matvec(link_of(0), re, im, False)
        put_right(right_w, nv, start, re, im)
        rows = pl.ds(start, TILE)
        for c in range(3):
            held_next[c, rows, :] = re[c]
            held_next[3 + c, rows, :] = im[c]

    def prepare_2(start):
        re, im = load(held_next, start)
        phased(left_w, nv, start, re, im, 58)
        re, im = load(held, start)
        put_right(right_v, nv, start, re, im)

    @pl.when(pl.program_id(0) == 0)
    def _():
        copies = collect(blocks, held, sems) + collect(next_blocks, held_next, next_sems)
        for copy in copies:
            copy.wait()

        def body(step, carry):
            prepare_1(pl.multiple_of(step * TILE, TILE))
            return carry

        lax.fori_loop(0, nv // TILE, body, 0)

        def tile_of(cols):
            forward[:, cols] = product(left_v, right_w, cols)

        tiles(nv, tile_of, prepare_2)

        def tile_of(cols):
            total = forward[:, cols] + product(left_w, right_v, cols)
            if has_acc:
                total = total + acc_ref[:, cols]
            if last:
                finish(mine_ref, total, cols, outs[0], outs[1])
            else:
                outs[0][:, cols] = total

        tiles(nv, tile_of)


def chunk_call(kind, mine, coef, blocks, others, acc, last, shard, packed=False):
    n_vec = len(blocks)
    nv = n_vec * blocks[0].shape[1]
    has_acc = acc is not None
    dirs = 2 if kind == "plane" else 1
    whole = lambda shape: pl.BlockSpec(shape, lambda i: (0,) * len(shape))
    if dirs == 2:
        shape = (2, 2 * nv, 2 * nv)
        tile = pl.BlockSpec((1, 2 * nv, 2 * nv), lambda i: (i, 0, 0))
        body = functools.partial(plane_kernel, n_vec, has_acc, last, packed, nv)
    else:
        shape = (2 * nv, 2 * nv)
        tile = pl.BlockSpec(shape, lambda i: (0, 0))
        body = functools.partial(cross_kernel, n_vec, has_acc, last, nv)
    args = [mine, coef] + blocks + others + ([acc] if has_acc else [])
    specs = [pl.BlockSpec(memory_space=pltpu.SMEM), whole(coef.shape)]
    specs += [pl.BlockSpec(memory_space=pl.ANY)] * (2 * n_vec)
    specs += [tile] if has_acc else []
    if last:
        half = (nv // shard, shard, 2 * nv)
        out_shape = [jax.ShapeDtypeStruct(half, F32)] * (2 * dirs)
        out_specs = [whole(half)] * (2 * dirs)
    else:
        out_shape = [jax.ShapeDtypeStruct(shape, F32)]
        out_specs = [tile]
    wide = 6 * LANES
    row_parts = 3 if packed else 6
    if dirs == 2:
        scratch = [
            pltpu.VMEM((6, nv, LANES), F32),
            pltpu.VMEM((row_parts, nv, LANES), F32),
            pltpu.VMEM((2, 2 * nv, wide), BF16),
            pltpu.VMEM((2, 2 * nv, wide // 2), BF16),
            pltpu.VMEM((2, 2 * nv, wide), BF16),
            pltpu.VMEM((2, 2 * nv, wide), BF16),
            pltpu.VMEM((2, 2 * nv, wide // 2), BF16),
        ]
    else:
        scratch = [pltpu.VMEM((6, nv, LANES), F32)] * 2
        scratch += [pltpu.VMEM((2, 2 * nv, wide), BF16)] * 4
        scratch += [pltpu.VMEM((2 * nv, 2 * nv), F32)]
    scratch += [pltpu.SemaphoreType.DMA((n_vec,))] * 2
    flops = 3 * 2 * 4 * nv * nv * wide * 2
    return pl.pallas_call(
        body,
        out_shape=out_shape,
        grid=(dirs,),
        in_specs=specs,
        out_specs=out_specs,
        scratch_shapes=scratch,
        input_output_aliases={2 + 2 * n_vec: 0} if has_acc and not last else {},
        cost_estimate=pl.CostEstimate(
            flops=flops, bytes_accessed=24 * nv * nv, transcendentals=0
        ),
        compiler_params=pltpu.CompilerParams(vmem_limit_bytes=32 * 1024 * 1024),
    )(*args)


def cut_kernel(count, index_ref, *refs):
    for x_ref, o_ref in zip(refs[:count], refs[count:]):
        o_ref[...] = x_ref[...]


def cut(vectors, index):
    count = index.shape[0]
    block = vectors.shape[:4] + (LANES,)
    piece = jax.ShapeDtypeStruct(block, F32)
    outs = pl.pallas_call(
        functools.partial(cut_kernel, count),
        out_shape=[piece] * count,
        grid_spec=pltpu.PrefetchScalarGridSpec(
            num_scalar_prefetch=1,
            grid=(1,),
            in_specs=[
                pl.BlockSpec(block, lambda i, at, k=k: (0, 0, 0, 0, at[k]))
                for k in range(count)
            ],
            out_specs=[pl.BlockSpec(block, lambda i, at: (0,) * 5)] * count,
        ),
        compiler_params=pltpu.CompilerParams(vmem_limit_bytes=32 * 1024 * 1024),
        name="cut",
    )(index, *([vectors] * count))
    return [o.reshape(6, block[2], LANES) for o in outs]


def phase_rows(momenta, xcoord, sites, extent_x, plane_y):
    ycoord = sites // PLANE_Z
    zcoord = sites % PLANE_Z
    p0, p1, p2 = (momenta[:, i][:, None] for i in range(3))
    frac = (p0 * xcoord % extent_x).astype(F32) / extent_x
    frac = frac + (p1 * ycoord[None] % plane_y).astype(F32) / plane_y
    frac = frac + (p2 * zcoord[None] % PLANE_Z).astype(F32) / PLANE_Z
    theta = 2.0 * jnp.pi * frac
    return jnp.cos(theta), jnp.sin(theta)


def coefficients(links, momenta, xcoord, start, subs, extent_x, plane):
    plane_y = plane // PLANE_Z
    width = subs * LANES
    rows = lax.dynamic_slice_in_dim(links.reshape(54, plane), start, width, 1)
    sites = start + jnp.arange(width, dtype=jnp.int32)
    cos, sin = phase_rows(momenta, xcoord, sites, extent_x, plane_y)
    cos_x, sin_x = phase_rows(momenta, xcoord + 1, sites, extent_x, plane_y)
    after = jnp.arange(subs, dtype=jnp.int32)[:, None] * LANES + LANES
    after = start + after + jnp.arange(LANES, dtype=jnp.int32)[None] % PLANE_Z
    cos_r, sin_r = phase_rows(
        momenta, xcoord, after.reshape(-1) % plane, extent_x, plane_y
    )
    low = jnp.arange(width) % LANES < PLANE_Z
    parts = [rows]
    for m in range(2):
        parts += [cos[m : m + 1], sin[m : m + 1]]
    for m in range(2):
        parts += [-cos_x[m : m + 1], -sin_x[m : m + 1]]
    for m in range(2):
        c, s = cos_r[m : m + 1], sin_r[m : m + 1]
        parts += [
            jnp.where(low, c, s),
            jnp.where(low, -s, c),
        ]
    parts.append(jnp.zeros((6, width), F32))
    table = jnp.concatenate(parts, 0)
    return [table[:, i * LANES : (i + 1) * LANES] for i in range(subs)]


def scatter_step(value, axis_dim, mine, axis, bit, size):
    keep = lax.dynamic_index_in_dim(value, mine, axis_dim, keepdims=False)
    send = lax.dynamic_index_in_dim(value, 1 - mine, axis_dim, keepdims=False)
    return keep + lax.ppermute(send, axis, xor_pairs(size, bit))


def reduce_block(keep, send, order, n_space, n_vec):
    s = lax.axis_index("space")
    t = lax.axis_index("vec")
    s_bits, v_bits = bits_of(n_space), bits_of(n_vec)
    lead, nv = (2,), keep.shape[-1] // 2
    value = keep + lax.ppermute(send, "space", xor_pairs(n_space, 1))
    left = list(range(s_bits - 1))
    value = value.reshape(lead + (2,) * len(left) + (nv // n_space, 2 * nv))
    for level in order:
        mine = (s >> (s_bits - 1 - level)) & 1
        if level < v_bits:
            mine = mine ^ ((t >> (v_bits - 1 - level)) & 1)
        value = scatter_step(
            value, len(lead) + left.index(level), mine, "space", 1 << (s_bits - 1 - level), n_space
        )
        left.remove(level)
    for level in range(v_bits):
        value = value.reshape(lead + (nv // n_space, 2, -1, 2, nv // n_vec))
        sent = lax.ppermute(value[..., 1, :], "vec", xor_pairs(n_vec, 1 << level))
        value = value[..., 0, :] + sent
    return value.reshape(lead + (nv // n_space, 2, nv // n_vec))


def on_device(vectors, links, momenta, directions):
    n_space, n_vec = lax.axis_size("space"), lax.axis_size("vec")
    s, t = lax.axis_index("space"), lax.axis_index("vec")
    own = vectors.shape[2]
    plane = vectors.shape[4]
    chunk = plane // n_vec
    subs = chunk // LANES
    nv = own * n_vec
    shard = nv // n_space
    down = [(i, (i - 1) % n_space) for i in range(n_space)]
    to_all = lambda part: [
        lax.ppermute(part[k], "vec", xor_pairs(n_vec, k)) for k in range(1, n_vec)
    ]
    order = list(reversed(range(subs)))
    partner = t ^ jnp.arange(n_vec, dtype=jnp.int32)
    first = jnp.concatenate([partner * subs + order[0], (partner + 1) % n_vec * subs])
    pieces = {}
    cuts = cut(vectors, first)
    pieces[order[0]], rows = cuts[:n_vec], cuts[n_vec:]
    rows = [
        jnp.concatenate([r[:3, :, :PLANE_Z], r[3:, :, :PLANE_Z]], 2) for r in rows
    ]
    got = {order[0]: to_all(pieces[order[0]])}
    rows = [rows[0]] + to_all(rows)
    rest = jnp.concatenate([partner * subs + sub for sub in order[1:]])
    cuts = cut(vectors, rest)
    for step, sub in enumerate(order[1:], 1):
        pieces[sub] = cuts[(step - 1) * n_vec : step * n_vec]
        got[sub] = to_all(pieces[sub])
    tables = coefficients(links, momenta, s, t * chunk, subs, n_space * vectors.shape[3], plane)
    mine = (s & 1).reshape(1).astype(jnp.int32)
    plane_acc = cross_acc = None
    for step, sub in enumerate(order):
        last = step == subs - 1
        blocks = [pieces[sub][0]] + got[sub]
        ahead = [lax.ppermute(x, "space", down) for x in blocks]
        planes = chunk_call(
            "plane", mine, tables[sub], blocks, rows, plane_acc, last, shard, step == 0
        )
        crosses = chunk_call(
            "cross", mine, tables[sub], blocks, ahead, cross_acc, last, shard
        )
        plane_acc, cross_acc = planes[0], crosses[0]
        rows = blocks
    forward = list(reversed(range(bits_of(n_space) - 1)))
    backward = forward[::-1]
    out = [
        reduce_block(*crosses, forward, n_space, n_vec),
        reduce_block(*planes[:2], forward, n_space, n_vec),
        reduce_block(*planes[2:], backward, n_space, n_vec),
    ]
    out = jnp.transpose(jnp.stack(out, 0), (0, 1, 3, 2, 4))
    out = [lax.dynamic_index_in_dim(out, directions[k], 0, keepdims=False) for k in range(3)]
    return jnp.stack(out, 1)


def solution(mesh):
    placed = (
        P(None, None, "vec", "space", None),
        P(None, None, None, None, "space", None),
        P(),
        P(),
    )
    return jax.shard_map(
        on_device,
        mesh=mesh,
        in_specs=placed,
        out_specs=P(None, None, None, "space", "vec"),
        check_vma=False,
    )
```
